32 devices in a mesh: outer: 8 (over z, x), inner: 4 (over y, core).
Axes of the slice: x: 2, y: 2, z: 4, core: 2. Of those that a mesh axis runs over, the one named last changes fastest.
Arguments:
- user_factors: float32 [16384, 256], P(('outer', 'inner')), may hold values from -0.3 to 0.3
- item_factors: float32 [16384, 256], P(('outer', 'inner')), may hold values from -0.3 to 0.3
- ratings: bfloat16 [16384, 8, 512], P(('outer', 'inner')), may hold values from -6 to 6
- weights: bfloat16 [16384, 8, 512], P(('outer', 'inner')), may hold values from 0 to 2, as said below
- tile_list: int32 [32, 8, 4], P(('outer', 'inner')), may hold values from 0 to 3, as said below
- tile_count: int32 [32, 8], P(('outer', 'inner')), may hold values from 1 to 4, as said below
Outputs:
- users_out: float32 [16384, 256], P(('outer', 'inner'))
- items_out: float32 [16384, 256], P(('outer', 'inner'))
The draws below stay inside these ranges and needn't reach their ends.
Inputs may be any that keep to these rules, and one draw needn't show every extreme that they name: Every row tile_list[d,k,:] names each of 0 to 3 once. `tile_count`: in every draw some device lists all 4 tiles in some stratum. `weights`: zero outside the listed tiles and at unobserved entries; elsewhere between 0.5 and 2.
All inputs are finite; a program needn't handle non-finite values.
Results may differ from the reference program's by a relative error of at most 0.003.
Values sent between devices are 32-bit elements; how exact they have to be, the bound alone decides.
No kernel may reach another device: no remote copies, remote signals or barrier semaphores. Data moves between devices by JAX's collectives and lax.ppermute only.
A program may use at most 64 MiB of HBM per device.

```python
import jax
import jax.numpy as jnp

R = 256
UD = 512
IB = 512
S_OUT = 2
S_IN = 4
TILES = 4
STRATA = 8
DEVS = 32
USERS = 16384
ITEMS = 16384
N_OUTER = 8
N_INNER = 4


def plan_tiles(key):
    base_key = jax.random.fold_in(key, 7101)
    raw_draw = jax.random.randint(jax.random.fold_in(base_key, 1), (DEVS, STRATA), 0, 16)
    counts = 1 + raw_draw * raw_draw * TILES // 256
    pick_dev = jax.random.randint(jax.random.fold_in(base_key, 2), (), 0, DEVS)
    pick_stratum = jax.random.randint(jax.random.fold_in(base_key, 3), (), 0, STRATA)
    forced = (jnp.arange(DEVS)[:, None] == pick_dev) & (jnp.arange(STRATA)[None, :] == pick_stratum)
    counts = jnp.where(forced, TILES, counts).astype(jnp.int32)
    scores = jax.random.randint(jax.random.fold_in(base_key, 4), (DEVS, STRATA, TILES), 0, 1 << 20) * TILES + jnp.arange(TILES)
    tile_order = jnp.argsort(scores, axis=-1).astype(jnp.int32)
    return (counts, tile_order)


def draw_tile_count(key, part):
    return plan_tiles(key)[0]


def draw_tile_list(key, part):
    return plan_tiles(key)[1]


def draw_weights(key, part):
    counts, tile_order = plan_tiles(key)
    slot_ids = jnp.arange(TILES, dtype=jnp.int32)
    in_list = slot_ids[None, None, :] < counts[:, :, None]
    matched = (tile_order[..., :, None] == slot_ids[None, None, None, :]) & in_list[..., :, None]
    listed = jnp.any(matched, axis=-2).astype(jnp.float32)
    listed = jnp.repeat(listed, IB // TILES, axis=-1)
    observed = jax.random.randint(jax.random.fold_in(key, 8101), (DEVS, UD, STRATA, IB), 0, 2).astype(jnp.float32)
    conf_key = jax.random.fold_in(key, 8102)
    confidence = jax.random.uniform(conf_key, (DEVS, UD, STRATA, IB), jnp.float32, 0.5, 2.0)
    weight = confidence * observed * listed[:, None, :, :]
    return weight.reshape(USERS, STRATA, IB).astype(jnp.bfloat16)


def level_of(key, extent, pieces, least, top_value):
    loudness, own = 1.0, jax.random.fold_in(key, 6)
    for dim, shards_of in pieces:
        draws = jnp.exp(jax.random.uniform(jax.random.fold_in(own, dim), (shards_of,), jnp.float32, least / len(pieces), top_value / len(pieces)))
        loudness = loudness * jnp.repeat(draws, extent[dim] // shards_of).reshape([-1 if axis == dim else 1 for axis in range(len(extent))])
    return loudness


def noise(key, dims, width, most, shards=(), kind=jnp.bfloat16):
    drawn = width * jax.random.normal(key, dims, jnp.float32)
    if shards:
        drawn = drawn * level_of(key, dims, shards, -0.22, 0.18)
    return jnp.clip(drawn, -most, most).astype(kind)


def setup_inputs(seed: int = 0) -> dict:
    arg_keys = jax.random.split(jax.random.key(seed), 7)
    user_factors = jnp.clip(jax.random.uniform(arg_keys[0], (USERS, R), jnp.float32, -0.3, 0.3) * level_of(arg_keys[0], (USERS, R), ((0, 32),), -0.4, 0.0), -0.3, 0.3)
    item_factors = jnp.clip(jax.random.uniform(arg_keys[1], (ITEMS, R), jnp.float32, -0.3, 0.3) * level_of(arg_keys[1], (ITEMS, R), ((0, 32),), -0.4, 0.0), -0.3, 0.3)
    ratings = noise(arg_keys[2], (USERS, STRATA, IB), 1.0, 6.0, ((0, 32),))
    weights = draw_weights(jax.random.fold_in(arg_keys[6], 71), 0)
    tile_list = draw_tile_list(jax.random.fold_in(arg_keys[6], 71), 0)
    tile_count = draw_tile_count(jax.random.fold_in(arg_keys[6], 71), 0)
    return {"user_factors": user_factors, "item_factors": item_factors, "ratings": ratings, "weights": weights, "tile_list": tile_list, "tile_count": tile_count}


learn_rate = 0.015
ridge_weight = 0.05


def listed_columns(tile_list, tile_count):
    slot_ids = jnp.arange(TILES, dtype=jnp.int32)
    in_list = slot_ids[None, :] < tile_count[:, None]
    matched = (tile_list[:, :, None] == slot_ids[None, None, :]) & in_list[:, :, None]
    listed = jnp.any(matched, axis=1).astype(jnp.float32)
    return jnp.repeat(listed, IB // TILES, axis=1)


def reference(user_factors, item_factors, ratings, weights, tile_list, tile_count):
    user_rows = user_factors.reshape(DEVS, UD, R)
    item_rows = item_factors.reshape(DEVS, IB, R)
    for outer_step in range(S_OUT):
        for inner_step in range(S_IN):
            stratum = outer_step * S_IN + inner_step
            tile_mask = listed_columns(tile_list[:, stratum, :], tile_count[:, stratum])
            rating = ratings[:, stratum, :].reshape(DEVS, UD, IB).astype(jnp.float32)
            weight = weights[:, stratum, :].reshape(DEVS, UD, IB).astype(jnp.float32)
            user_half = user_rows.astype(jnp.bfloat16).astype(jnp.float32)
            item_half = item_rows.astype(jnp.bfloat16).astype(jnp.float32)
            predicted = jnp.einsum("dur,dir->dui", user_half, item_half)
            residual = (weight * (predicted - rating) * tile_mask[:, None, :]).astype(jnp.bfloat16).astype(jnp.float32)
            grad_users = jnp.einsum("dui,dir->dur", residual, item_half)
            grad_items = jnp.einsum("dui,dur->dir", residual, user_half)
            user_rows = user_rows - learn_rate * (grad_users + ridge_weight * user_rows)
            item_rows = item_rows - learn_rate * (grad_items + ridge_weight * item_rows)
            grouped = item_rows.reshape(N_OUTER, N_INNER, IB, R)
            if inner_step < S_IN - 1:
                grouped = jnp.roll(grouped, 1, axis=1)
            elif outer_step < S_OUT - 1:
                grouped = jnp.roll(grouped, 1, axis=0)
            item_rows = grouped.reshape(DEVS, IB, R)
    return user_rows.reshape(USERS, R), item_rows.reshape(ITEMS, R)
```

```python
import jax
import jax.numpy as jnp
from jax import lax
from jax.experimental import pallas as pl
from jax.experimental.pallas import tpu as pltpu
from jax.sharding import PartitionSpec as P

S_OUT = 2
S_IN = 4
PIECES = 4
USER_CHUNK = 32

learn_rate = 0.015
ridge_weight = 0.05


def from_behind(value, axis, steps):
    count = lax.axis_size(axis)
    pairs = [(source, (source + steps) % count) for source in range(count)]
    return lax.ppermute(value, axis, pairs)


def move_items(item_rows, outer_step, inner_step):
    if inner_step < S_IN - 1:
        return from_behind(item_rows, "inner", 1)
    if outer_step < S_OUT - 1:
        return from_behind(item_rows, "outer", 1)
    return item_rows


def sort_strata(ratings, weights, tile_list, tile_count):
    users, strata, items = ratings.shape
    tiles = tile_list.shape[2]
    width = items // tiles
    chunk = USER_CHUNK
    rows = chunk * strata

    def kernel(list_ref, count_ref, rating_ref, weight_ref, *outs):
        rating_outs, weight_outs = outs[:strata], outs[strata:]
        target = lax.broadcasted_iota(jnp.int32, (rows, rows), 0)
        source = lax.broadcasted_iota(jnp.int32, (rows, rows), 1)
        wanted = (target % chunk) * strata + target // chunk
        pick = jnp.where(source == wanted, 1.0, 0.0).astype(jnp.bfloat16)
        rating = jnp.dot(pick, rating_ref[...], preferred_element_type=jnp.float32)
        weight = jnp.dot(pick, weight_ref[...], preferred_element_type=jnp.float32)
        for stratum in range(strata):
            part = slice(stratum * chunk, (stratum + 1) * chunk)
            rating_outs[stratum][...] = rating[part].astype(jnp.bfloat16)
            for tile in range(tiles):
                listed = jnp.float32(0.0)
                for slot in range(tiles):
                    hit = (list_ref[stratum, slot] == tile) & (slot < count_ref[stratum])
                    listed = jnp.where(hit, 1.0, listed)
                cols = slice(tile * width, (tile + 1) * width)
                weight_outs[stratum][:, cols] = (weight[part, cols] * listed).astype(jnp.bfloat16)

    spec_in = pl.BlockSpec((rows, items), lambda step, *_: (step, 0))
    spec_out = pl.BlockSpec((chunk, items), lambda step, *_: (step, 0))
    shape = jax.ShapeDtypeStruct((users, items), jnp.bfloat16)
    size = users * strata * items * 2
    outs = pl.pallas_call(
        kernel,
        grid_spec=pltpu.PrefetchScalarGridSpec(
            num_scalar_prefetch=2,
            grid=(users // chunk,),
            in_specs=[spec_in, spec_in],
            out_specs=[spec_out] * (2 * strata),
        ),
        out_shape=[shape] * (2 * strata),
        compiler_params=pltpu.CompilerParams(vmem_limit_bytes=16 * 1024 * 1024),
        cost_estimate=pl.CostEstimate(flops=4 * size * rows, bytes_accessed=4 * size, transcendentals=0),
        name="sort_strata",
    )(tile_list[0], tile_count[0], ratings.reshape(users * strata, items), weights.reshape(users * strata, items))
    return outs[:strata], outs[strata:]


def local(user_factors, item_factors, ratings, weights, tile_list, tile_count):
    items = item_factors.shape[0]
    m = items // PIECES
    rating_of, weight_of = sort_strata(ratings, weights, tile_list, tile_count)
    user_rows = user_factors
    pieces = [item_factors[j * m : (j + 1) * m] for j in range(PIECES)]
    contract_rank = (((1,), (1,)), ((), ()))
    contract_users = (((0,), (0,)), ((), ()))
    f32 = jnp.float32
    for outer_step in range(S_OUT):
        for inner_step in range(S_IN):
            stratum = outer_step * S_IN + inner_step
            user_half = user_rows.astype(jnp.bfloat16)
            moved = []
            grad_users = ridge_weight * user_rows
            for j in range(PIECES):
                cols = slice(j * m, (j + 1) * m)
                rating = rating_of[stratum][:, cols].astype(f32)
                weight = weight_of[stratum][:, cols].astype(f32)
                piece = pieces[j]
                half = piece.astype(jnp.bfloat16)
                predicted = lax.dot_general(user_half, half, contract_rank, preferred_element_type=f32)
                residual = (weight * (predicted - rating)).astype(jnp.bfloat16)
                grad_items = lax.dot_general(residual, user_half, contract_users, preferred_element_type=f32)
                new_piece = piece - learn_rate * (grad_items + ridge_weight * piece)
                moved.append(move_items(new_piece, outer_step, inner_step))
                grad_users = grad_users + jnp.dot(residual, half, preferred_element_type=f32)
            user_rows = user_rows - learn_rate * grad_users
            pieces = moved
    return (user_rows, jnp.concatenate(pieces, axis=0))


def solution(mesh):
    in_specs = (
        P(("outer", "inner"), None),
        P(("outer", "inner"), None),
        P(("outer", "inner"), None, None),
        P(("outer", "inner"), None, None),
        P(("outer", "inner"), None, None),
        P(("outer", "inner"), None),
    )
    out_specs = (P(("outer", "inner"), None), P(("outer", "inner"), None))
    return jax.shard_map(local, mesh=mesh, in_specs=in_specs, out_specs=out_specs, check_vma=False)
```

```python
import jax
import jax.numpy as jnp
from jax import lax
from jax.experimental import pallas as pl
from jax.experimental.pallas import tpu as pltpu
from jax.sharding import PartitionSpec as P

S_OUT = 2
S_IN = 4
PIECES = 4
CHUNK = 32
PARTS = 4

learn_rate = 0.015
ridge_weight = 0.05


VMEM = pl.BlockSpec(memory_space=pltpu.VMEM)
HBM = pl.BlockSpec(memory_space=pltpu.HBM)
LIMIT = 24 * 1024 * 1024
RANK = (((1,), (1,)), ((), ()))
USERS = (((0,), (0,)), ((), ()))
f32 = jnp.float32
bf16 = jnp.bfloat16


def from_behind(value, axis, steps):
    count = lax.axis_size(axis)
    pairs = [(source, (source + steps) % count) for source in range(count)]
    return lax.ppermute(value, axis, pairs)


def move_items(item_rows, outer_step, inner_step):
    if inner_step < S_IN - 1:
        return from_behind(item_rows, "inner", 1)
    if outer_step < S_OUT - 1:
        return from_behind(item_rows, "outer", 1)
    return item_rows


def call(kernel, out_shape, in_specs, out_specs, flops, name, scratch=()):
    return pl.pallas_call(
        kernel,
        out_shape=out_shape,
        in_specs=in_specs,
        out_specs=out_specs,
        scratch_shapes=scratch,
        compiler_params=pltpu.CompilerParams(vmem_limit_bytes=LIMIT),
        cost_estimate=pl.CostEstimate(flops=flops, bytes_accessed=1024, transcendentals=0),
        name=name,
    )


def load(user_factors, item_factors, ratings, weights, tile_list, tile_count):
    users, strata, items = ratings.shape
    rank = item_factors.shape[1]
    tiles = tile_list.shape[2]
    width = items // tiles
    rows = CHUNK * strata
    part_users = users // PARTS
    m = items // PIECES

    def kernel(
        list_hbm, count_hbm, user_hbm, item_hbm, rating_hbm, weight_hbm,
        rating_out, weight_out, user_out, half_out, *refs,
    ):
        pieces, (raw, lists, counts, sems, small) = refs[:PIECES], refs[PIECES:]
        tables = [
            pltpu.make_async_copy(list_hbm, lists, small.at[0]),
            pltpu.make_async_copy(count_hbm, counts, small.at[1]),
        ]
        factors = [pltpu.make_async_copy(user_hbm, user_out, small.at[2])] + [
            pltpu.make_async_copy(item_hbm.at[pl.ds(j * m, m)], pieces[j], small.at[3 + j]) for j in range(PIECES)
        ]
        copies = []
        for p in range(PARTS):
            part = pl.ds(p * part_users * strata, part_users * strata)
            copies.append(
                [
                    pltpu.make_async_copy(source.at[part], raw.at[side, part], sems.at[side, p])
                    for side, source in enumerate((rating_hbm, weight_hbm))
                ]
            )
        for copy in tables + factors + sum(copies, []):
            copy.start()
        target = lax.broadcasted_iota(jnp.int32, (rows, rows), 0)
        source = lax.broadcasted_iota(jnp.int32, (rows, rows), 1)
        wanted = (target % CHUNK) * strata + target // CHUNK
        pick = jnp.where(source == wanted, 1.0, 0.0).astype(bf16)
        for copy in tables:
            copy.wait()
        listed = []
        for stratum in range(strata):
            for tile in range(tiles):
                on = jnp.float32(0.0)
                for slot in range(tiles):
                    hit = (lists[slot, stratum] == tile) & (slot < counts[0, stratum])
                    on = jnp.where(hit, 1.0, on)
                listed.append(on)
        for copy in factors:
            copy.wait()
        half_out[...] = user_out[...].astype(bf16)
        for p in range(PARTS):
            for copy in copies[p]:
                copy.wait()
            for first in range(p * part_users, (p + 1) * part_users, CHUNK):
                mine = slice(first * strata, first * strata + rows)
                into = slice(first, first + CHUNK)
                rating = jnp.dot(pick, raw[0, mine, :], preferred_element_type=f32)
                for stratum in range(strata):
                    part = rating[stratum * CHUNK : (stratum + 1) * CHUNK]
                    rating_out[stratum, into, :] = part.astype(bf16)
                weight = jnp.dot(pick, raw[1, mine, :], preferred_element_type=f32)
                for stratum in range(strata):
                    for tile in range(tiles):
                        cols = slice(tile * width, (tile + 1) * width)
                        part = weight[stratum * CHUNK : (stratum + 1) * CHUNK, cols]
                        part = part * listed[stratum * tiles + tile]
                        weight_out[stratum, into, cols] = part.astype(bf16)

    table = jax.ShapeDtypeStruct((strata, users, items), bf16)
    outs = call(
        kernel,
        (
            table,
            table,
            jax.ShapeDtypeStruct((users, rank), f32),
            jax.ShapeDtypeStruct((users, rank), bf16),
            *[jax.ShapeDtypeStruct((m, rank), f32)] * PIECES,
        ),
        [HBM] * 6,
        (VMEM,) * (4 + PIECES),
        4 * users * strata * items * rows,
        "load",
        [
            pltpu.VMEM((2, users * strata, items), bf16),
            pltpu.SMEM((tiles, strata), jnp.int32),
            pltpu.SMEM((1, strata), jnp.int32),
            pltpu.SemaphoreType.DMA((2, PARTS)),
            pltpu.SemaphoreType.DMA((3 + PIECES,)),
        ],
    )(
        *[
            pltpu.with_memory_space_constraint(value, pltpu.HBM)
            for value in (
                tile_list[0].T,
                tile_count,
                user_factors,
                item_factors,
                ratings.reshape(users * strata, items),
                weights.reshape(users * strata, items),
            )
        ]
    )
    return *outs[:4], list(outs[4:])


def residual_of(user_half, half, rating_ref, weight_ref, stratum, cols):
    predicted = lax.dot_general(user_half, half, RANK, preferred_element_type=f32)
    rating = rating_ref[stratum, :, cols].astype(f32)
    weight = weight_ref[stratum, :, cols].astype(f32)
    return (weight * (predicted - rating)).astype(bf16)


def step_items(rows, residual, user_half):
    grad = lax.dot_general(residual, user_half, USERS, preferred_element_type=f32)
    return rows - learn_rate * (grad + ridge_weight * rows)


def item_step(stratum, j, user_half, piece, ratings, weights):
    m, rank = piece.shape
    users = user_half.shape[0]
    cols = slice(j * m, (j + 1) * m)

    def kernel(user_ref, piece_ref, rating_ref, weight_ref, new_ref, residual_ref):
        rows = piece_ref[...]
        residual = residual_of(user_ref[...], rows.astype(bf16), rating_ref, weight_ref, stratum, cols)
        residual_ref[...] = residual
        new_ref[...] = step_items(rows, residual, user_ref[...])

    return call(
        kernel,
        (jax.ShapeDtypeStruct((m, rank), f32), jax.ShapeDtypeStruct((users, m), bf16)),
        [VMEM] * 4,
        (VMEM, VMEM),
        4 * users * m * rank,
        f"item_step_{stratum}_{j}",
    )(user_half, piece, ratings, weights)


def user_step(stratum, user_rows, residuals, pieces):
    count = len(pieces)

    def kernel(user_ref, *refs):
        residual_refs, piece_refs, (new_ref, half_ref) = refs[:count], refs[count : 2 * count], refs[2 * count :]
        rows = user_ref[...]
        grad = ridge_weight * rows
        for residual_ref, piece_ref in zip(residual_refs, piece_refs):
            grad += jnp.dot(residual_ref[...], piece_ref[...].astype(bf16), preferred_element_type=f32)
        rows = rows - learn_rate * grad
        new_ref[...] = rows
        half_ref[...] = rows.astype(bf16)

    users, rank = user_rows.shape
    return call(
        kernel,
        (jax.ShapeDtypeStruct((users, rank), f32), jax.ShapeDtypeStruct((users, rank), bf16)),
        [VMEM] * (1 + 2 * count),
        (VMEM, VMEM),
        2 * users * rank * sum(piece.shape[0] for piece in pieces),
        f"user_step_{stratum}",
    )(user_rows, *residuals, *pieces)


def last_step(stratum, user_rows, user_half, pieces, new_pieces, residuals, ratings, weights):
    done = len(new_pieces)
    m, rank = pieces[0].shape
    users = user_rows.shape[0]
    cols = slice(done * m, (done + 1) * m)

    def kernel(user_ref, half_ref, rating_ref, weight_ref, *refs):
        piece_refs, new_refs = refs[: done + 1], refs[done + 1 : 2 * done + 1]
        residual_refs = refs[2 * done + 1 : 3 * done + 1]
        users_out, items_out, last_items, last_users, sems = refs[3 * done + 1 :]
        copies = [
            pltpu.make_async_copy(new_refs[j], items_out.at[pl.ds(j * m, m)], sems.at[j]) for j in range(done)
        ]
        for copy in copies:
            copy.start()
        rows = piece_refs[done][...]
        half = rows.astype(bf16)
        residual = residual_of(half_ref[...], half, rating_ref, weight_ref, stratum, cols)
        user = user_ref[...]
        grad = ridge_weight * user
        for j in range(done):
            grad += jnp.dot(residual_refs[j][...], piece_refs[j][...].astype(bf16), preferred_element_type=f32)
        grad += jnp.dot(residual, half, preferred_element_type=f32)
        last_users[...] = user - learn_rate * grad
        copies.append(pltpu.make_async_copy(last_users, users_out, sems.at[done + 1]))
        copies[-1].start()
        last_items[...] = step_items(rows, residual, half_ref[...])
        copies.append(pltpu.make_async_copy(last_items, items_out.at[pl.ds(done * m, m)], sems.at[done]))
        copies[-1].start()
        for copy in copies:
            copy.wait()

    return call(
        kernel,
        (jax.ShapeDtypeStruct((users, rank), f32), jax.ShapeDtypeStruct(((done + 1) * m, rank), f32)),
        [VMEM] * (4 + 3 * done + 1),
        (HBM, HBM),
        4 * users * m * rank,
        "last_step",
        [
            pltpu.VMEM((m, rank), f32),
            pltpu.VMEM((users, rank), f32),
            pltpu.SemaphoreType.DMA((done + 2,)),
        ],
    )(user_rows, user_half, ratings, weights, *pieces, *new_pieces, *residuals)


def local(user_factors, item_factors, ratings, weights, tile_list, tile_count):
    ratings, weights, user_rows, user_half, pieces = load(
        user_factors, item_factors, ratings, weights, tile_list, tile_count
    )
    for outer_step in range(S_OUT):
        for inner_step in range(S_IN):
            stratum = outer_step * S_IN + inner_step
            last = stratum == S_OUT * S_IN - 1
            moved, residuals, news = [], [], []
            for j in range(PIECES - 1 if last else PIECES):
                new_piece, residual = item_step(stratum, j, user_half, pieces[j], ratings, weights)
                news.append(new_piece)
                moved.append(move_items(new_piece, outer_step, inner_step))
                residuals.append(residual)
            if last:
                return last_step(stratum, user_rows, user_half, pieces, news, residuals, ratings, weights)
            user_rows, user_half = user_step(stratum, user_rows, residuals, pieces)
            pieces = moved


def solution(mesh):
    in_specs = (
        P(("outer", "inner"), None),
        P(("outer", "inner"), None),
        P(("outer", "inner"), None, None),
        P(("outer", "inner"), None, None),
        P(("outer", "inner"), None, None),
        P(("outer", "inner"), None),
    )
    out_specs = (P(("outer", "inner"), None), P(("outer", "inner"), None))
    return jax.shard_map(local, mesh=mesh, in_specs=in_specs, out_specs=out_specs, check_vma=False)
```

```python
import jax
import jax.numpy as jnp
from jax import lax
from jax.experimental import pallas as pl
from jax.experimental.pallas import tpu as pltpu
from jax.sharding import PartitionSpec as P


S_OUT = 2
S_IN = 4
SHARES = (1, 1, 1, 1)
LATER = ((2, 3, 4), (5, 6, 7))
CHUNK = 32
GROUP = 128
LANES = 128

learn_rate = 0.015
ridge_weight = 0.05


VMEM = pl.BlockSpec(memory_space=pltpu.VMEM)
HBM = pl.BlockSpec(memory_space=pltpu.HBM)
LIMIT = 24 * 1024 * 1024
RANK = (((1,), (1,)), ((), ()))
USERS = (((0,), (0,)), ((), ()))
f32 = jnp.float32
bf16 = jnp.bfloat16


def from_behind(value, axis, steps):
    count = lax.axis_size(axis)
    pairs = [(source, (source + steps) % count) for source in range(count)]
    return lax.ppermute(value, axis, pairs)


def move_items(item_rows, outer_step, inner_step):
    if inner_step < S_IN - 1:
        return from_behind(item_rows, "inner", 1)
    if outer_step < S_OUT - 1:
        return from_behind(item_rows, "outer", 1)
    return item_rows


def call(kernel, out_shape, in_specs, out_specs, flops, scratch=()):
    return pl.pallas_call(
        kernel,
        out_shape=out_shape,
        in_specs=in_specs,
        out_specs=out_specs,
        scratch_shapes=scratch,
        compiler_params=pltpu.CompilerParams(vmem_limit_bytes=LIMIT),
        cost_estimate=pl.CostEstimate(flops=flops, bytes_accessed=1024, transcendentals=0),
    )


def cut(items):
    unit = items // sum(SHARES)
    return [unit * sum(SHARES[:j]) for j in range(len(SHARES))], [unit * share for share in SHARES]


def hbm(value):
    return pltpu.with_memory_space_constraint(value, pltpu.HBM)


def load(user_factors, item_factors, ratings, weights, tile_list, tile_count):
    users, strata, items = ratings.shape
    rank = item_factors.shape[1]
    tiles = tile_list.shape[2]
    width = items // tiles
    starts, sizes = cut(items)
    count = len(sizes)
    blocks = items // LANES

    def view(table):
        table = table.reshape(users, strata, blocks, LANES).transpose(0, 2, 1, 3)
        return table.reshape(users, blocks, strata // 2, 2, LANES)

    def kernel(
        list_hbm, count_hbm, user_hbm, item_hbm, rating_hbm, weight_hbm,
        rating_out, weight_out, mask_out, user_out, half_out, *refs,
    ):
        pieces, (raw, lists, counts, sems, small) = refs[:count], refs[count:]
        tables = [
            pltpu.make_async_copy(list_hbm, lists, small.at[0]),
            pltpu.make_async_copy(count_hbm, counts, small.at[1]),
        ]
        factors = [pltpu.make_async_copy(user_hbm, user_out, small.at[2])] + [
            pltpu.make_async_copy(item_hbm.at[pl.ds(starts[j], sizes[j])], pieces[j], small.at[3 + j])
            for j in range(count)
        ]
        copies = [
            [
                pltpu.make_async_copy(source.at[:, block, 0], raw.at[side, block], sems.at[side, block])
                for block in range(blocks)
            ]
            for side, source in enumerate((rating_hbm, weight_hbm))
        ]
        for copy in tables + copies[0] + copies[1] + factors:
            copy.start()
        target = lax.broadcasted_iota(jnp.int32, (2 * GROUP, 2 * GROUP), 0)
        source = lax.broadcasted_iota(jnp.int32, (2 * GROUP, 2 * GROUP), 1)
        wanted = (target % GROUP) * 2 + target // GROUP
        pick = jnp.where(source == wanted, 1.0, 0.0).astype(bf16)
        for copy in tables:
            copy.wait()
        for stratum in range(strata):
            for tile in range(tiles):
                listed = jnp.float32(0.0)
                for slot in range(tiles):
                    hit = (lists[slot, stratum] == tile) & (slot < counts[0, stratum])
                    listed = jnp.where(hit, 1.0, listed)
                mask_out[stratum : stratum + 1, tile * width : (tile + 1) * width] = jnp.full((1, width), listed)
        for side, out in enumerate((rating_out, weight_out)):
            for copy in copies[side]:
                copy.wait()
            for block in range(blocks):
                pairs = raw.at[side, block].reshape(2 * users, LANES)
                cols = slice(block * LANES, (block + 1) * LANES)
                for first in range(0, users, GROUP):
                    rows = jnp.dot(pick, pairs[2 * first : 2 * (first + GROUP), :], preferred_element_type=f32)
                    for stratum in range(2):
                        part = rows[stratum * GROUP : (stratum + 1) * GROUP]
                        if side == 1:
                            part = part * mask_out[stratum : stratum + 1, cols]
                        out[stratum, first : first + GROUP, cols] = part.astype(bf16)
        for copy in factors:
            copy.wait()
        half_out[...] = user_out[...].astype(bf16)

    table = jax.ShapeDtypeStruct((2, users, items), bf16)
    outs = call(
        kernel,
        (
            table,
            table,
            jax.ShapeDtypeStruct((strata, items), f32),
            jax.ShapeDtypeStruct((users, rank), f32),
            jax.ShapeDtypeStruct((users, rank), bf16),
            *[jax.ShapeDtypeStruct((size, rank), f32) for size in sizes],
        ),
        [HBM] * 6,
        (VMEM,) * (5 + count),
        8 * users * items * GROUP,
        [
            pltpu.VMEM((2, blocks, users, 2, LANES), bf16),
            pltpu.SMEM((tiles, strata), jnp.int32),
            pltpu.SMEM((1, strata), jnp.int32),
            pltpu.SemaphoreType.DMA((2, blocks)),
            pltpu.SemaphoreType.DMA((3 + count,)),
        ],
    )(
        hbm(tile_list[0].T), hbm(tile_count), hbm(user_factors), hbm(item_factors),
        hbm(view(ratings)), hbm(view(weights)),
    )
    return *outs[:5], list(outs[5:])


def sort_strata(chosen, ratings, weights, mask):
    users, strata, items = ratings.shape
    rows = CHUNK * strata
    kept = len(chosen)

    def kernel(rating_ref, weight_ref, mask_ref, rating_out, weight_out):
        target = lax.broadcasted_iota(jnp.int32, (CHUNK * kept, rows), 0)
        source = lax.broadcasted_iota(jnp.int32, (CHUNK * kept, rows), 1)
        wanted = (target % CHUNK) * strata + target // CHUNK + chosen[0]
        pick = jnp.where(source == wanted, 1.0, 0.0).astype(bf16)
        for first in range(0, users, CHUNK):
            mine = slice(first * strata, first * strata + rows)
            into = slice(first, first + CHUNK)
            rating = jnp.dot(pick, rating_ref[mine, :], preferred_element_type=f32)
            weight = jnp.dot(pick, weight_ref[mine, :], preferred_element_type=f32)
            for index, stratum in enumerate(chosen):
                part = slice(index * CHUNK, (index + 1) * CHUNK)
                rating_out[index, into, :] = rating[part].astype(bf16)
                weight_out[index, into, :] = (weight[part] * mask_ref[stratum : stratum + 1, :]).astype(bf16)

    table = jax.ShapeDtypeStruct((kept, users, items), bf16)
    return call(
        kernel, (table, table), [VMEM] * 3, (VMEM, VMEM), 4 * kept * users * items * rows
    )(ratings.reshape(users * strata, items), weights.reshape(users * strata, items), mask)


def piece_step(user_half, rows, rating_ref, weight_ref, stratum, cols):
    predicted = lax.dot_general(user_half, rows.astype(bf16), RANK, preferred_element_type=f32)
    rating = rating_ref[stratum, :, cols].astype(f32)
    weight = weight_ref[stratum, :, cols].astype(f32)
    residual = (weight * (predicted - rating)).astype(bf16)
    grad = lax.dot_general(residual, user_half, USERS, preferred_element_type=f32)
    return residual, rows - learn_rate * (grad + ridge_weight * rows)


def users_grad(residual, rows):
    return jnp.dot(residual, rows.astype(bf16), preferred_element_type=f32)


def first_piece(stratum, cols, user_half, piece, ratings, weights):
    def kernel(half_ref, piece_ref, rating_ref, weight_ref, new_ref, residual_ref):
        residual_ref[...], new_ref[...] = piece_step(
            half_ref[...], piece_ref[...], rating_ref, weight_ref, stratum, cols
        )

    users = user_half.shape[0]
    m, rank = piece.shape
    return call(
        kernel,
        (jax.ShapeDtypeStruct((m, rank), f32), jax.ShapeDtypeStruct((users, m), bf16)),
        [VMEM] * 4,
        (VMEM, VMEM),
        4 * users * m * rank,
    )(user_half, piece, ratings, weights)


def middle_piece(stratum, cols, user_rows, user_half, piece, ratings, weights, earlier):
    def kernel(user_ref, half_ref, piece_ref, rating_ref, weight_ref, *refs):
        earlier_refs, (new_ref, grad_ref) = refs[:-2], refs[-2:]
        rows = piece_ref[...]
        residual, new_ref[...] = piece_step(half_ref[...], rows, rating_ref, weight_ref, stratum, cols)
        if len(earlier_refs) == 2:
            grad = ridge_weight * user_ref[...] + users_grad(earlier_refs[1][...], earlier_refs[0][...])
        else:
            grad = earlier_refs[0][...]
        grad_ref[...] = grad + users_grad(residual, rows)

    users = user_half.shape[0]
    m, rank = piece.shape
    return call(
        kernel,
        (jax.ShapeDtypeStruct((m, rank), f32), jax.ShapeDtypeStruct((users, rank), f32)),
        [VMEM] * (5 + len(earlier)),
        (VMEM, VMEM),
        8 * users * m * rank,
    )(user_rows, user_half, piece, ratings, weights, *earlier)


def last_piece(stratum, cols, user_rows, user_half, grad, piece, ratings, weights):
    def kernel(user_ref, half_ref, grad_ref, piece_ref, rating_ref, weight_ref, new_ref, user_out, half_out):
        rows = piece_ref[...]
        residual, new_ref[...] = piece_step(half_ref[...], rows, rating_ref, weight_ref, stratum, cols)
        user = user_ref[...] - learn_rate * (grad_ref[...] + users_grad(residual, rows))
        user_out[...] = user
        half_out[...] = user.astype(bf16)

    users = user_half.shape[0]
    m, rank = piece.shape
    return call(
        kernel,
        (
            jax.ShapeDtypeStruct((m, rank), f32),
            jax.ShapeDtypeStruct((users, rank), f32),
            jax.ShapeDtypeStruct((users, rank), bf16),
        ),
        [VMEM] * 6,
        (VMEM,) * 3,
        6 * users * m * rank,
    )(user_rows, user_half, grad, piece, ratings, weights)


def finish(stratum, cols, user_rows, user_half, grad, piece, ratings, weights, news):
    m, rank = piece.shape
    users = user_rows.shape[0]
    done = len(news)

    def kernel(user_ref, half_ref, grad_ref, piece_ref, rating_ref, weight_ref, *refs):
        new_refs, (users_out, items_out, last_items, last_users, sems) = refs[:done], refs[done:]
        copies = []

        def write(source, target):
            copies.append(pltpu.make_async_copy(source, target, sems.at[len(copies)]))
            copies[-1].start()

        start = 0
        for new_ref in new_refs:
            write(new_ref, items_out.at[pl.ds(start, new_ref.shape[0])])
            start += new_ref.shape[0]
        rows = piece_ref[...]
        residual, new_rows = piece_step(half_ref[...], rows, rating_ref, weight_ref, stratum, cols)
        last_users[...] = user_ref[...] - learn_rate * (grad_ref[...] + users_grad(residual, rows))
        write(last_users, users_out)
        last_items[...] = new_rows
        write(last_items, items_out.at[pl.ds(start, m)])
        for copy in copies:
            copy.wait()

    items = m + sum(new.shape[0] for new in news)
    return call(
        kernel,
        (jax.ShapeDtypeStruct((users, rank), f32), jax.ShapeDtypeStruct((items, rank), f32)),
        [VMEM] * (6 + done),
        (HBM, HBM),
        6 * users * m * rank,
        [
            pltpu.VMEM((m, rank), f32),
            pltpu.VMEM((users, rank), f32),
            pltpu.SemaphoreType.DMA((done + 2,)),
        ],
    )(user_rows, user_half, grad, piece, ratings, weights, *news)


def local(user_factors, item_factors, ratings, weights, tile_list, tile_count):
    starts, sizes = cut(item_factors.shape[0])
    cols = [slice(start, start + size) for start, size in zip(starts, sizes)]
    last = len(sizes) - 1
    rating_01, weight_01, mask, user_rows, user_half, pieces = load(
        user_factors, item_factors, ratings, weights, tile_list, tile_count
    )
    tables = [(0, rating_01, weight_01), (1, rating_01, weight_01)]
    for chosen in LATER:
        sorted_ratings, sorted_weights = sort_strata(chosen, ratings, weights, mask)
        tables.extend((index, sorted_ratings, sorted_weights) for index in range(len(chosen)))
    for outer_step in range(S_OUT):
        for inner_step in range(S_IN):
            stratum = outer_step * S_IN + inner_step
            row, rating, weight = tables[stratum]

            def move(new):
                return move_items(new, outer_step, inner_step)

            new, residual = first_piece(row, cols[0], user_half, pieces[0], rating, weight)
            news = [move(new)]
            earlier = (pieces[0], residual)
            for j in range(1, last):
                new, grad = middle_piece(row, cols[j], user_rows, user_half, pieces[j], rating, weight, earlier)
                news.append(move(new))
                earlier = (grad,)
            if stratum == S_OUT * S_IN - 1:
                return finish(
                    row, cols[last], user_rows, user_half, grad, pieces[last], rating, weight, news
                )
            new, user_rows, user_half = last_piece(
                row, cols[last], user_rows, user_half, grad, pieces[last], rating, weight
            )
            news.append(move(new))
            pieces = news


def solution(mesh):
    in_specs = (
        P(("outer", "inner"), None),
        P(("outer", "inner"), None),
        P(("outer", "inner"), None, None),
        P(("outer", "inner"), None, None),
        P(("outer", "inner"), None, None),
        P(("outer", "inner"), None),
    )
    out_specs = (P(("outer", "inner"), None), P(("outer", "inner"), None))

    return jax.shard_map(local, mesh=mesh, in_specs=in_specs, out_specs=out_specs, check_vma=False)
```

```python
import jax
import jax.numpy as jnp
from jax import lax
from jax.experimental import pallas as pl
from jax.experimental.pallas import tpu as pltpu
from jax.sharding import PartitionSpec as P


S_OUT = 2
S_IN = 4
SHARES = (1, 1, 1, 1)
LATER = ((2, 3, 4), (5, 6, 7))
CHUNK = 32
GROUP = 128
LANES = 128

learn_rate = 0.015
ridge_weight = 0.05


VMEM = pl.BlockSpec(memory_space=pltpu.VMEM)
HBM = pl.BlockSpec(memory_space=pltpu.HBM)
LIMIT = 24 * 1024 * 1024
RANK = (((1,), (1,)), ((), ()))
USERS = (((0,), (0,)), ((), ()))
f32 = jnp.float32
bf16 = jnp.bfloat16


def from_behind(value, axis, steps):
    count = lax.axis_size(axis)
    pairs = [(source, (source + steps) % count) for source in range(count)]
    return lax.ppermute(value, axis, pairs)


def move_items(item_rows, outer_step, inner_step):
    if inner_step < S_IN - 1:
        return from_behind(item_rows, "inner", 1)
    if outer_step < S_OUT - 1:
        return from_behind(item_rows, "outer", 1)
    return item_rows


def call(kernel, out_shape, in_specs, out_specs, flops, scratch=()):
    return pl.pallas_call(
        kernel,
        out_shape=out_shape,
        in_specs=in_specs,
        out_specs=out_specs,
        scratch_shapes=scratch,
        compiler_params=pltpu.CompilerParams(vmem_limit_bytes=LIMIT),
        cost_estimate=pl.CostEstimate(flops=flops, bytes_accessed=1024, transcendentals=0),
    )


def cut(items):
    unit = items // sum(SHARES)
    return [unit * sum(SHARES[:j]) for j in range(len(SHARES))], [unit * share for share in SHARES]


def hbm(value):
    return pltpu.with_memory_space_constraint(value, pltpu.HBM)


def load(user_factors, item_factors, ratings, weights, tile_list, tile_count):
    users, strata, items = ratings.shape
    rank = item_factors.shape[1]
    tiles = tile_list.shape[2]
    width = items // tiles
    starts, sizes = cut(items)
    count = len(sizes)
    blocks = items // LANES

    def view(table):
        table = table.reshape(users, strata, blocks, LANES).transpose(0, 2, 1, 3)
        return table.reshape(users, blocks, strata // 2, 2, LANES)

    def kernel(
        list_hbm, count_hbm, user_hbm, item_hbm, rating_hbm, weight_hbm,
        rating_out, weight_out, mask_out, user_out, half_out, *refs,
    ):
        pieces, (raw, lists, counts, sems, small) = refs[:count], refs[count:]
        tables = [
            pltpu.make_async_copy(list_hbm, lists, small.at[0]),
            pltpu.make_async_copy(count_hbm, counts, small.at[1]),
        ]
        factors = [pltpu.make_async_copy(user_hbm, user_out, small.at[2])] + [
            pltpu.make_async_copy(item_hbm.at[pl.ds(starts[j], sizes[j])], pieces[j], small.at[3 + j])
            for j in range(count)
        ]
        copies = [
            [
                pltpu.make_async_copy(source.at[:, block, 0], raw.at[side, block], sems.at[side, block])
                for block in range(blocks)
            ]
            for side, source in enumerate((rating_hbm, weight_hbm))
        ]
        for copy in tables + copies[0] + copies[1] + factors:
            copy.start()
        target = lax.broadcasted_iota(jnp.int32, (2 * GROUP, 2 * GROUP), 0)
        source = lax.broadcasted_iota(jnp.int32, (2 * GROUP, 2 * GROUP), 1)
        wanted = (target % GROUP) * 2 + target // GROUP
        pick = jnp.where(source == wanted, 1.0, 0.0).astype(bf16)
        for copy in tables:
            copy.wait()
        for stratum in range(strata):
            for tile in range(tiles):
                listed = jnp.float32(0.0)
                for slot in range(tiles):
                    hit = (lists[slot, stratum] == tile) & (slot < counts[0, stratum])
                    listed = jnp.where(hit, 1.0, listed)
                mask_out[stratum : stratum + 1, tile * width : (tile + 1) * width] = jnp.full((1, width), listed)
        for side, out in enumerate((rating_out, weight_out)):
            for copy in copies[side]:
                copy.wait()
            for block in range(blocks):
                pairs = raw.at[side, block].reshape(2 * users, LANES)
                cols = slice(block * LANES, (block + 1) * LANES)
                for first in range(0, users, GROUP):
                    rows = jnp.dot(pick, pairs[2 * first : 2 * (first + GROUP), :], preferred_element_type=f32)
                    for stratum in range(2):
                        part = rows[stratum * GROUP : (stratum + 1) * GROUP]
                        if side == 1:
                            part = part * mask_out[stratum : stratum + 1, cols]
                        out[stratum, first : first + GROUP, cols] = part.astype(bf16)
        for copy in factors:
            copy.wait()
        half_out[...] = user_out[...].astype(bf16)

    table = jax.ShapeDtypeStruct((2, users, items), bf16)
    outs = call(
        kernel,
        (
            table,
            table,
            jax.ShapeDtypeStruct((strata, items), f32),
            jax.ShapeDtypeStruct((users, rank), f32),
            jax.ShapeDtypeStruct((users, rank), bf16),
            *[jax.ShapeDtypeStruct((size, rank), f32) for size in sizes],
        ),
        [HBM] * 6,
        (VMEM,) * (5 + count),
        8 * users * items * GROUP,
        [
            pltpu.VMEM((2, blocks, users, 2, LANES), bf16),
            pltpu.SMEM((tiles, strata), jnp.int32),
            pltpu.SMEM((1, strata), jnp.int32),
            pltpu.SemaphoreType.DMA((2, blocks)),
            pltpu.SemaphoreType.DMA((3 + count,)),
        ],
    )(
        hbm(tile_list[0].T), hbm(tile_count), hbm(user_factors), hbm(item_factors),
        hbm(view(ratings)), hbm(view(weights)),
    )
    return *outs[:5], list(outs[5:])


def sort_strata(chosen, ratings, weights, mask):
    users, strata, items = ratings.shape
    rows = CHUNK * strata
    kept = len(chosen)

    def kernel(rating_ref, weight_ref, mask_ref, rating_out, weight_out):
        target = lax.broadcasted_iota(jnp.int32, (CHUNK * kept, rows), 0)
        source = lax.broadcasted_iota(jnp.int32, (CHUNK * kept, rows), 1)
        wanted = (target % CHUNK) * strata + target // CHUNK + chosen[0]
        pick = jnp.where(source == wanted, 1.0, 0.0).astype(bf16)
        for first in range(0, users, CHUNK):
            mine = slice(first * strata, first * strata + rows)
            into = slice(first, first + CHUNK)
            rating = jnp.dot(pick, rating_ref[mine, :], preferred_element_type=f32)
            weight = jnp.dot(pick, weight_ref[mine, :], preferred_element_type=f32)
            for index, stratum in enumerate(chosen):
                part = slice(index * CHUNK, (index + 1) * CHUNK)
                rating_out[index, into, :] = rating[part].astype(bf16)
                weight_out[index, into, :] = (weight[part] * mask_ref[stratum : stratum + 1, :]).astype(bf16)

    table = jax.ShapeDtypeStruct((kept, users, items), bf16)
    return call(
        kernel, (table, table), [VMEM] * 3, (VMEM, VMEM), 4 * kept * users * items * rows
    )(ratings.reshape(users * strata, items), weights.reshape(users * strata, items), mask)


def piece_step(user_half, rows, rating_ref, weight_ref, stratum, cols):
    predicted = lax.dot_general(user_half, rows.astype(bf16), RANK, preferred_element_type=f32)
    rating = rating_ref[stratum, :, cols].astype(f32)
    weight = weight_ref[stratum, :, cols].astype(f32)
    residual = (weight * (predicted - rating)).astype(bf16)
    grad = lax.dot_general(residual, user_half, USERS, preferred_element_type=f32)
    return residual, rows - learn_rate * (grad + ridge_weight * rows)


def users_grad(residual, rows):
    return jnp.dot(residual, rows.astype(bf16), preferred_element_type=f32)


def first_piece(stratum, cols, user_half, piece, ratings, weights):
    def kernel(half_ref, piece_ref, rating_ref, weight_ref, new_ref, residual_ref):
        residual_ref[...], new_ref[...] = piece_step(
            half_ref[...], piece_ref[...], rating_ref, weight_ref, stratum, cols
        )

    users = user_half.shape[0]
    m, rank = piece.shape
    return call(
        kernel,
        (jax.ShapeDtypeStruct((m, rank), f32), jax.ShapeDtypeStruct((users, m), bf16)),
        [VMEM] * 4,
        (VMEM, VMEM),
        4 * users * m * rank,
    )(user_half, piece, ratings, weights)


def users_step(user_rows, residuals, pieces):
    count = len(pieces)

    def kernel(user_ref, *refs):
        residual_refs, piece_refs, (user_out, half_out) = refs[:count], refs[count : 2 * count], refs[2 * count :]
        user = user_ref[...]
        grad = ridge_weight * user
        for residual_ref, piece_ref in zip(residual_refs, piece_refs):
            grad += users_grad(residual_ref[...], piece_ref[...])
        user = user - learn_rate * grad
        user_out[...] = user
        half_out[...] = user.astype(bf16)

    users, rank = user_rows.shape
    return call(
        kernel,
        (jax.ShapeDtypeStruct((users, rank), f32), jax.ShapeDtypeStruct((users, rank), bf16)),
        [VMEM] * (1 + 2 * count),
        (VMEM, VMEM),
        2 * users * rank * users,
    )(user_rows, *residuals, *pieces)


def middle_piece(stratum, cols, user_rows, user_half, piece, ratings, weights, earlier):
    def kernel(user_ref, half_ref, piece_ref, rating_ref, weight_ref, *refs):
        earlier_refs, (new_ref, grad_ref) = refs[:-2], refs[-2:]
        rows = piece_ref[...]
        residual, new_ref[...] = piece_step(half_ref[...], rows, rating_ref, weight_ref, stratum, cols)
        if len(earlier_refs) == 2:
            grad = ridge_weight * user_ref[...] + users_grad(earlier_refs[1][...], earlier_refs[0][...])
        else:
            grad = earlier_refs[0][...]
        grad_ref[...] = grad + users_grad(residual, rows)

    users = user_half.shape[0]
    m, rank = piece.shape
    return call(
        kernel,
        (jax.ShapeDtypeStruct((m, rank), f32), jax.ShapeDtypeStruct((users, rank), f32)),
        [VMEM] * (5 + len(earlier)),
        (VMEM, VMEM),
        8 * users * m * rank,
    )(user_rows, user_half, piece, ratings, weights, *earlier)


def finish(stratum, cols, user_rows, user_half, grad, piece, ratings, weights, news):
    m, rank = piece.shape
    users = user_rows.shape[0]
    done = len(news)

    def kernel(user_ref, half_ref, grad_ref, piece_ref, rating_ref, weight_ref, *refs):
        new_refs, (users_out, items_out, last_items, last_users, sems) = refs[:done], refs[done:]
        copies = []

        def write(source, target):
            copies.append(pltpu.make_async_copy(source, target, sems.at[len(copies)]))
            copies[-1].start()

        start = 0
        for new_ref in new_refs:
            write(new_ref, items_out.at[pl.ds(start, new_ref.shape[0])])
            start += new_ref.shape[0]
        rows = piece_ref[...]
        residual, new_rows = piece_step(half_ref[...], rows, rating_ref, weight_ref, stratum, cols)
        last_users[...] = user_ref[...] - learn_rate * (grad_ref[...] + users_grad(residual, rows))
        write(last_users, users_out)
        last_items[...] = new_rows
        write(last_items, items_out.at[pl.ds(start, m)])
        for copy in copies:
            copy.wait()

    items = m + sum(new.shape[0] for new in news)
    return call(
        kernel,
        (jax.ShapeDtypeStruct((users, rank), f32), jax.ShapeDtypeStruct((items, rank), f32)),
        [VMEM] * (6 + done),
        (HBM, HBM),
        6 * users * m * rank,
        [
            pltpu.VMEM((m, rank), f32),
            pltpu.VMEM((users, rank), f32),
            pltpu.SemaphoreType.DMA((done + 2,)),
        ],
    )(user_rows, user_half, grad, piece, ratings, weights, *news)


def local(user_factors, item_factors, ratings, weights, tile_list, tile_count):
    starts, sizes = cut(item_factors.shape[0])
    cols = [slice(start, start + size) for start, size in zip(starts, sizes)]
    last = len(sizes) - 1
    rating_01, weight_01, mask, user_rows, user_half, pieces = load(
        user_factors, item_factors, ratings, weights, tile_list, tile_count
    )
    tables = [(0, rating_01, weight_01), (1, rating_01, weight_01)]
    for chosen in LATER:
        sorted_ratings, sorted_weights = sort_strata(chosen, ratings, weights, mask)
        tables.extend((index, sorted_ratings, sorted_weights) for index in range(len(chosen)))
    for outer_step in range(S_OUT):
        for inner_step in range(S_IN):
            stratum = outer_step * S_IN + inner_step
            row, rating, weight = tables[stratum]

            def move(new):
                return move_items(new, outer_step, inner_step)

            final = stratum == S_OUT * S_IN - 1
            news, residuals = [], []
            if final:
                new, residual = first_piece(row, cols[0], user_half, pieces[0], rating, weight)
                news = [new]
                earlier = (pieces[0], residual)
                for j in range(1, last):
                    new, grad = middle_piece(row, cols[j], user_rows, user_half, pieces[j], rating, weight, earlier)
                    news.append(new)
                    earlier = (grad,)
                return finish(row, cols[last], user_rows, user_half, grad, pieces[last], rating, weight, news)
            for j in range(last + 1):
                new, residual = first_piece(row, cols[j], user_half, pieces[j], rating, weight)
                residuals.append(residual)
                news.append(move(new))
            user_rows, user_half = users_step(user_rows, residuals, pieces)
            pieces = news


def solution(mesh):
    in_specs = (
        P(("outer", "inner"), None),
        P(("outer", "inner"), None),
        P(("outer", "inner"), None, None),
        P(("outer", "inner"), None, None),
        P(("outer", "inner"), None, None),
        P(("outer", "inner"), None),
    )
    out_specs = (P(("outer", "inner"), None), P(("outer", "inner"), None))

    return jax.shard_map(local, mesh=mesh, in_specs=in_specs, out_specs=out_specs, check_vma=False)
```

```python
import jax
import jax.numpy as jnp
from jax import lax
from jax.experimental import pallas as pl
from jax.experimental.pallas import tpu as pltpu
from jax.sharding import PartitionSpec as P


S_OUT = 2
S_IN = 4
SHARES = (1, 1, 1, 1)
LATER = ((2, 3, 4), (5, 6, 7))
CHUNK = 32
GROUP = 128
LANES = 128

learn_rate = 0.015
ridge_weight = 0.05


VMEM = pl.BlockSpec(memory_space=pltpu.VMEM)
HBM = pl.BlockSpec(memory_space=pltpu.HBM)
LIMIT = 24 * 1024 * 1024
RANK = (((1,), (1,)), ((), ()))
USERS = (((0,), (0,)), ((), ()))
f32 = jnp.float32
bf16 = jnp.bfloat16


def from_behind(value, axis, steps):
    count = lax.axis_size(axis)
    pairs = [(source, (source + steps) % count) for source in range(count)]
    return lax.ppermute(value, axis, pairs)


def move_items(item_rows, outer_step, inner_step):
    if inner_step < S_IN - 1:
        return from_behind(item_rows, "inner", 1)
    if outer_step < S_OUT - 1:
        return from_behind(item_rows, "outer", 1)
    return item_rows


def call(kernel, out_shape, in_specs, out_specs, flops, scratch=()):
    return pl.pallas_call(
        kernel,
        out_shape=out_shape,
        in_specs=in_specs,
        out_specs=out_specs,
        scratch_shapes=scratch,
        compiler_params=pltpu.CompilerParams(vmem_limit_bytes=LIMIT),
        cost_estimate=pl.CostEstimate(flops=flops, bytes_accessed=1024, transcendentals=0),
    )


def cut(items):
    unit = items // sum(SHARES)
    return [unit * sum(SHARES[:j]) for j in range(len(SHARES))], [unit * share for share in SHARES]


def hbm(value):
    return pltpu.with_memory_space_constraint(value, pltpu.HBM)


def load(user_factors, item_factors, ratings, weights, tile_list, tile_count):
    users, strata, items = ratings.shape
    rank = item_factors.shape[1]
    tiles = tile_list.shape[2]
    width = items // tiles
    starts, sizes = cut(items)
    count = len(sizes)
    blocks = items // LANES

    def view(table):
        table = table.reshape(users, strata, blocks, LANES).transpose(0, 2, 1, 3)
        return table.reshape(users, blocks, strata // 2, 2, LANES)

    def kernel(
        list_hbm, count_hbm, user_hbm, item_hbm, rating_hbm, weight_hbm,
        rating_out, weight_out, mask_out, user_out, half_out, new_out, residual_out, *refs,
    ):
        pieces, (raw, lists, counts, sems, small) = refs[:count], refs[count:]
        tables = [
            pltpu.make_async_copy(list_hbm, lists, small.at[0]),
            pltpu.make_async_copy(count_hbm, counts, small.at[1]),
        ]
        factors = [pltpu.make_async_copy(user_hbm, user_out, small.at[2])] + [
            pltpu.make_async_copy(item_hbm.at[pl.ds(starts[j], sizes[j])], pieces[j], small.at[3 + j])
            for j in range(count)
        ]
        copies = [
            [
                pltpu.make_async_copy(source.at[:, block, 0], raw.at[side, block], sems.at[side, block])
                for side, source in enumerate((rating_hbm, weight_hbm))
            ]
            for block in range(blocks)
        ]
        ahead = sizes[0] // LANES
        for copy in tables + sum(copies[:ahead], []) + factors[:2] + sum(copies[ahead:], []) + factors[2:]:
            copy.start()
        target = lax.broadcasted_iota(jnp.int32, (2 * GROUP, 2 * GROUP), 0)
        source = lax.broadcasted_iota(jnp.int32, (2 * GROUP, 2 * GROUP), 1)
        wanted = (target % GROUP) * 2 + target // GROUP
        pick = jnp.where(source == wanted, 1.0, 0.0).astype(bf16)
        for copy in tables:
            copy.wait()
        for stratum in range(strata):
            for tile in range(tiles):
                listed = jnp.float32(0.0)
                for slot in range(tiles):
                    hit = (lists[slot, stratum] == tile) & (slot < counts[0, stratum])
                    listed = jnp.where(hit, 1.0, listed)
                mask_out[stratum : stratum + 1, tile * width : (tile + 1) * width] = jnp.full((1, width), listed)

        def sort(some):
            for block in some:
                for copy in copies[block]:
                    copy.wait()
            for block in some:
                cols = slice(block * LANES, (block + 1) * LANES)
                for side, out in enumerate((rating_out, weight_out)):
                    pairs = raw.at[side, block].reshape(2 * users, LANES)
                    for first in range(0, users, GROUP):
                        rows = jnp.dot(pick, pairs[2 * first : 2 * (first + GROUP), :], preferred_element_type=f32)
                        for stratum in range(2):
                            part = rows[stratum * GROUP : (stratum + 1) * GROUP]
                            if side == 1:
                                part = part * mask_out[stratum : stratum + 1, cols]
                            out[stratum, first : first + GROUP, cols] = part.astype(bf16)

        sort(range(ahead))
        for copy in factors[:2]:
            copy.wait()
        half_out[...] = user_out[...].astype(bf16)
        residual_out[...], new_out[...] = piece_step(
            half_out[...], pieces[0][...], rating_out, weight_out, 0, slice(0, sizes[0])
        )
        sort(range(ahead, blocks))
        for copy in factors[2:]:
            copy.wait()

    table = jax.ShapeDtypeStruct((2, users, items), bf16)
    outs = call(
        kernel,
        (
            table,
            table,
            jax.ShapeDtypeStruct((strata, items), f32),
            jax.ShapeDtypeStruct((users, rank), f32),
            jax.ShapeDtypeStruct((users, rank), bf16),
            jax.ShapeDtypeStruct((sizes[0], rank), f32),
            jax.ShapeDtypeStruct((users, sizes[0]), bf16),
            *[jax.ShapeDtypeStruct((size, rank), f32) for size in sizes],
        ),
        [HBM] * 6,
        (VMEM,) * (7 + count),
        8 * users * items * GROUP,
        [
            pltpu.VMEM((2, blocks, users, 2, LANES), bf16),
            pltpu.SMEM((tiles, strata), jnp.int32),
            pltpu.SMEM((1, strata), jnp.int32),
            pltpu.SemaphoreType.DMA((2, blocks)),
            pltpu.SemaphoreType.DMA((3 + count,)),
        ],
    )(
        hbm(tile_list[0].T), hbm(tile_count), hbm(user_factors), hbm(item_factors),
        hbm(view(ratings)), hbm(view(weights)),
    )
    return *outs[:7], list(outs[7:])


def sort_strata(chosen, ratings, weights, mask):
    users, strata, items = ratings.shape
    rows = CHUNK * strata
    kept = len(chosen)

    def kernel(rating_ref, weight_ref, mask_ref, rating_out, weight_out):
        target = lax.broadcasted_iota(jnp.int32, (CHUNK * kept, rows), 0)
        source = lax.broadcasted_iota(jnp.int32, (CHUNK * kept, rows), 1)
        wanted = (target % CHUNK) * strata + target // CHUNK + chosen[0]
        pick = jnp.where(source == wanted, 1.0, 0.0).astype(bf16)
        for first in range(0, users, CHUNK):
            mine = slice(first * strata, first * strata + rows)
            into = slice(first, first + CHUNK)
            rating = jnp.dot(pick, rating_ref[mine, :], preferred_element_type=f32)
            weight = jnp.dot(pick, weight_ref[mine, :], preferred_element_type=f32)
            for index, stratum in enumerate(chosen):
                part = slice(index * CHUNK, (index + 1) * CHUNK)
                rating_out[index, into, :] = rating[part].astype(bf16)
                weight_out[index, into, :] = (weight[part] * mask_ref[stratum : stratum + 1, :]).astype(bf16)

    table = jax.ShapeDtypeStruct((kept, users, items), bf16)
    return call(
        kernel, (table, table), [VMEM] * 3, (VMEM, VMEM), 4 * kept * users * items * rows
    )(ratings.reshape(users * strata, items), weights.reshape(users * strata, items), mask)


def piece_step(user_half, rows, rating_ref, weight_ref, stratum, cols):
    predicted = lax.dot_general(user_half, rows.astype(bf16), RANK, preferred_element_type=f32)
    rating = rating_ref[stratum, :, cols].astype(f32)
    weight = weight_ref[stratum, :, cols].astype(f32)
    residual = (weight * (predicted - rating)).astype(bf16)
    grad = lax.dot_general(residual, user_half, USERS, preferred_element_type=f32)
    return residual, rows - learn_rate * (grad + ridge_weight * rows)


def users_grad(residual, rows):
    return jnp.dot(residual, rows.astype(bf16), preferred_element_type=f32)


def first_piece(stratum, cols, user_half, piece, ratings, weights):
    def kernel(half_ref, piece_ref, rating_ref, weight_ref, new_ref, residual_ref):
        residual_ref[...], new_ref[...] = piece_step(
            half_ref[...], piece_ref[...], rating_ref, weight_ref, stratum, cols
        )

    users = user_half.shape[0]
    m, rank = piece.shape
    return call(
        kernel,
        (jax.ShapeDtypeStruct((m, rank), f32), jax.ShapeDtypeStruct((users, m), bf16)),
        [VMEM] * 4,
        (VMEM, VMEM),
        4 * users * m * rank,
    )(user_half, piece, ratings, weights)


def users_step(user_rows, residuals, pieces):
    count = len(pieces)

    def kernel(user_ref, *refs):
        residual_refs, piece_refs, (user_out, half_out) = refs[:count], refs[count : 2 * count], refs[2 * count :]
        user = user_ref[...]
        grad = ridge_weight * user
        for residual_ref, piece_ref in zip(residual_refs, piece_refs):
            grad += users_grad(residual_ref[...], piece_ref[...])
        user = user - learn_rate * grad
        user_out[...] = user
        half_out[...] = user.astype(bf16)

    users, rank = user_rows.shape
    return call(
        kernel,
        (jax.ShapeDtypeStruct((users, rank), f32), jax.ShapeDtypeStruct((users, rank), bf16)),
        [VMEM] * (1 + 2 * count),
        (VMEM, VMEM),
        2 * users * rank * users,
    )(user_rows, *residuals, *pieces)


def middle_piece(stratum, cols, user_rows, user_half, piece, ratings, weights, earlier):
    def kernel(user_ref, half_ref, piece_ref, rating_ref, weight_ref, *refs):
        earlier_refs, (new_ref, grad_ref) = refs[:-2], refs[-2:]
        rows = piece_ref[...]
        residual, new_ref[...] = piece_step(half_ref[...], rows, rating_ref, weight_ref, stratum, cols)
        if len(earlier_refs) == 2:
            grad = ridge_weight * user_ref[...] + users_grad(earlier_refs[1][...], earlier_refs[0][...])
        else:
            grad = earlier_refs[0][...]
        grad_ref[...] = grad + users_grad(residual, rows)

    users = user_half.shape[0]
    m, rank = piece.shape
    return call(
        kernel,
        (jax.ShapeDtypeStruct((m, rank), f32), jax.ShapeDtypeStruct((users, rank), f32)),
        [VMEM] * (5 + len(earlier)),
        (VMEM, VMEM),
        8 * users * m * rank,
    )(user_rows, user_half, piece, ratings, weights, *earlier)


def finish(stratum, cols, user_rows, user_half, grad, piece, ratings, weights, news):
    m, rank = piece.shape
    users = user_rows.shape[0]
    done = len(news)

    def kernel(user_ref, half_ref, grad_ref, piece_ref, rating_ref, weight_ref, *refs):
        new_refs, (users_out, items_out, last_items, last_users, sems) = refs[:done], refs[done:]
        copies = []

        def write(source, target):
            copies.append(pltpu.make_async_copy(source, target, sems.at[len(copies)]))
            copies[-1].start()

        start = 0
        for new_ref in new_refs:
            write(new_ref, items_out.at[pl.ds(start, new_ref.shape[0])])
            start += new_ref.shape[0]
        rows = piece_ref[...]
        residuals = []
        for part in range(2):
            mine = slice(part * users // 2, (part + 1) * users // 2)
            predicted = lax.dot_general(half_ref[mine, :], rows.astype(bf16), RANK, preferred_element_type=f32)
            rating = rating_ref[stratum, mine, cols].astype(f32)
            weight = weight_ref[stratum, mine, cols].astype(f32)
            residuals.append((weight * (predicted - rating)).astype(bf16))
            last_users[mine, :] = user_ref[mine, :] - learn_rate * (
                grad_ref[mine, :] + users_grad(residuals[-1], rows)
            )
            span = pl.ds(part * users // 2, users // 2)
            write(last_users.at[span], users_out.at[span])
        residual = jnp.concatenate(residuals, axis=0)
        grad = lax.dot_general(residual, half_ref[...], USERS, preferred_element_type=f32)
        last_items[...] = rows - learn_rate * (grad + ridge_weight * rows)
        write(last_items, items_out.at[pl.ds(start, m)])
        for copy in copies:
            copy.wait()

    items = m + sum(new.shape[0] for new in news)
    return call(
        kernel,
        (jax.ShapeDtypeStruct((users, rank), f32), jax.ShapeDtypeStruct((items, rank), f32)),
        [VMEM] * (6 + done),
        (HBM, HBM),
        6 * users * m * rank,
        [
            pltpu.VMEM((m, rank), f32),
            pltpu.VMEM((users, rank), f32),
            pltpu.SemaphoreType.DMA((done + 3,)),
        ],
    )(user_rows, user_half, grad, piece, ratings, weights, *news)


def local(user_factors, item_factors, ratings, weights, tile_list, tile_count):
    starts, sizes = cut(item_factors.shape[0])
    cols = [slice(start, start + size) for start, size in zip(starts, sizes)]
    last = len(sizes) - 1
    rating_01, weight_01, mask, user_rows, user_half, *opened, pieces = load(
        user_factors, item_factors, ratings, weights, tile_list, tile_count
    )
    tables = [(0, rating_01, weight_01), (1, rating_01, weight_01)]
    for chosen in LATER:
        sorted_ratings, sorted_weights = sort_strata(chosen, ratings, weights, mask)
        tables.extend((index, sorted_ratings, sorted_weights) for index in range(len(chosen)))
    for outer_step in range(S_OUT):
        for inner_step in range(S_IN):
            stratum = outer_step * S_IN + inner_step
            row, rating, weight = tables[stratum]

            def move(new):
                return move_items(new, outer_step, inner_step)

            final = stratum == S_OUT * S_IN - 1
            news, residuals = [], []
            if final:
                new, residual = first_piece(row, cols[0], user_half, pieces[0], rating, weight)
                news = [new]
                earlier = (pieces[0], residual)
                for j in range(1, last):
                    new, grad = middle_piece(row, cols[j], user_rows, user_half, pieces[j], rating, weight, earlier)
                    news.append(new)
                    earlier = (grad,)
                return finish(row, cols[last], user_rows, user_half, grad, pieces[last], rating, weight, news)
            for j in range(last + 1):
                if stratum == 0 and j == 0:
                    new, residual = opened
                else:
                    new, residual = first_piece(row, cols[j], user_half, pieces[j], rating, weight)
                residuals.append(residual)
                news.append(move(new))
            user_rows, user_half = users_step(user_rows, residuals, pieces)
            pieces = news


def solution(mesh):
    in_specs = (
        P(("outer", "inner"), None),
        P(("outer", "inner"), None),
        P(("outer", "inner"), None, None),
        P(("outer", "inner"), None, None),
        P(("outer", "inner"), None, None),
        P(("outer", "inner"), None),
    )
    out_specs = (P(("outer", "inner"), None), P(("outer", "inner"), None))

    return jax.shard_map(local, mesh=mesh, in_specs=in_specs, out_specs=out_specs, check_vma=False)
```

```python
import jax
import jax.numpy as jnp
from jax import lax
from jax.experimental import pallas as pl
from jax.experimental.pallas import tpu as pltpu
from jax.sharding import PartitionSpec as P


S_OUT = 2
S_IN = 4
SHARES = (1, 1, 1, 1)
LATER = ((2, 3), (4, 5, 6, 7))
CHUNK = 32
GROUP = 128
LANES = 128

learn_rate = 0.015
ridge_weight = 0.05


VMEM = pl.BlockSpec(memory_space=pltpu.VMEM)
HBM = pl.BlockSpec(memory_space=pltpu.HBM)
LIMIT = 24 * 1024 * 1024
RANK = (((1,), (1,)), ((), ()))
USERS = (((0,), (0,)), ((), ()))
f32 = jnp.float32
bf16 = jnp.bfloat16


def from_behind(value, axis, steps):
    count = lax.axis_size(axis)
    pairs = [(source, (source + steps) % count) for source in range(count)]
    return lax.ppermute(value, axis, pairs)


def move_items(item_rows, outer_step, inner_step):
    if inner_step < S_IN - 1:
        return from_behind(item_rows, "inner", 1)
    if outer_step < S_OUT - 1:
        return from_behind(item_rows, "outer", 1)
    return item_rows


def call(kernel, out_shape, in_specs, out_specs, flops, scratch=()):
    return pl.pallas_call(
        kernel,
        out_shape=out_shape,
        in_specs=in_specs,
        out_specs=out_specs,
        scratch_shapes=scratch,
        compiler_params=pltpu.CompilerParams(vmem_limit_bytes=LIMIT),
        cost_estimate=pl.CostEstimate(flops=flops, bytes_accessed=1024, transcendentals=0),
    )


def cut(items):
    unit = items // sum(SHARES)
    return [unit * sum(SHARES[:j]) for j in range(len(SHARES))], [unit * share for share in SHARES]


def hbm(value):
    return pltpu.with_memory_space_constraint(value, pltpu.HBM)


def sort_pairs(some, raw, mask, rating_out, weight_out):
    users = rating_out.shape[1]
    target = lax.broadcasted_iota(jnp.int32, (2 * GROUP, 2 * GROUP), 0)
    source = lax.broadcasted_iota(jnp.int32, (2 * GROUP, 2 * GROUP), 1)
    wanted = (target % GROUP) * 2 + target // GROUP
    pick = jnp.where(source == wanted, 1.0, 0.0).astype(bf16)
    for block in some:
        cols = slice(block * LANES, (block + 1) * LANES)
        for side, out in enumerate((rating_out, weight_out)):
            pairs = raw.at[side, block].reshape(2 * users, LANES)
            for first in range(0, users, GROUP):
                rows = jnp.dot(pick, pairs[2 * first : 2 * (first + GROUP), :], preferred_element_type=f32)
                for stratum in range(2):
                    part = rows[stratum * GROUP : (stratum + 1) * GROUP]
                    if side == 1:
                        part = part * mask[stratum : stratum + 1, cols]
                    out[stratum, first : first + GROUP, cols] = part.astype(bf16)


def sort_rest(raw, mask, ratings, weights, ahead, after):
    def kernel(raw_ref, mask_ref, rating_in, weight_in, after_ref, rating_out, weight_out):
        @pl.when(lax.axis_index("inner") % 2 == 0)
        def _():
            sort_pairs(range(ahead, raw_ref.shape[1]), raw_ref, mask_ref, rating_out, weight_out)

    table = jax.ShapeDtypeStruct(ratings.shape, bf16)
    return pl.pallas_call(
        kernel,
        out_shape=(table, table),
        in_specs=[VMEM] * 4 + [pl.BlockSpec(memory_space=pl.ANY)],
        out_specs=(VMEM, VMEM),
        input_output_aliases={2: 0, 3: 1},
        compiler_params=pltpu.CompilerParams(vmem_limit_bytes=LIMIT),
        cost_estimate=pl.CostEstimate(flops=1024, bytes_accessed=1024, transcendentals=0),
        name="sort_rest",
    )(raw, mask, ratings, weights, after)


def load(user_factors, item_factors, ratings, weights, tile_list, tile_count):
    users, strata, items = ratings.shape
    rank = item_factors.shape[1]
    tiles = tile_list.shape[2]
    width = items // tiles
    starts, sizes = cut(items)
    count = len(sizes)
    blocks = items // LANES

    def view(table):
        table = table.reshape(users, strata, blocks, LANES).transpose(0, 2, 1, 3)
        return table.reshape(users, blocks, strata // 2, 2, LANES)

    def kernel(
        list_hbm, count_hbm, user_hbm, item_hbm, rating_hbm, weight_hbm,
        rating_out, weight_out, mask_out, user_out, half_out, new_out, residual_out, raw, *refs,
    ):
        pieces, (lists, counts, sems, small) = refs[:count], refs[count:]
        tables = [
            pltpu.make_async_copy(list_hbm, lists, small.at[0]),
            pltpu.make_async_copy(count_hbm, counts, small.at[1]),
        ]
        factors = [pltpu.make_async_copy(user_hbm, user_out, small.at[2])] + [
            pltpu.make_async_copy(item_hbm.at[pl.ds(starts[j], sizes[j])], pieces[j], small.at[3 + j])
            for j in range(count)
        ]
        copies = [
            [
                pltpu.make_async_copy(source.at[:, block, 0], raw.at[side, block], sems.at[side, block])
                for side, source in enumerate((rating_hbm, weight_hbm))
            ]
            for block in range(blocks)
        ]
        ahead = sizes[0] // LANES
        for copy in tables + sum(copies[:ahead], []) + factors[:2] + sum(copies[ahead:], []) + factors[2:]:
            copy.start()
        for copy in tables:
            copy.wait()
        for stratum in range(strata):
            for tile in range(tiles):
                listed = jnp.float32(0.0)
                for slot in range(tiles):
                    hit = (lists[slot, stratum] == tile) & (slot < counts[0, stratum])
                    listed = jnp.where(hit, 1.0, listed)
                mask_out[stratum : stratum + 1, tile * width : (tile + 1) * width] = jnp.full((1, width), listed)

        for copy in sum(copies[:ahead], []):
            copy.wait()
        sort_pairs(range(ahead), raw, mask_out, rating_out, weight_out)
        for copy in factors[:2]:
            copy.wait()
        half_out[...] = user_out[...].astype(bf16)
        residual_out[...], new_out[...] = piece_step(
            half_out[...], pieces[0][...], rating_out, weight_out, 0, slice(0, sizes[0])
        )
        for copy in sum(copies[ahead:], []) + factors[2:]:
            copy.wait()

        sort_pairs(range(ahead, 2 * ahead), raw, mask_out, rating_out, weight_out)

        @pl.when(lax.axis_index("inner") % 2 == 1)
        def _():
            sort_pairs(range(2 * ahead, blocks), raw, mask_out, rating_out, weight_out)

    table = jax.ShapeDtypeStruct((2, users, items), bf16)
    outs = call(
        kernel,
        (
            table,
            table,
            jax.ShapeDtypeStruct((strata, items), f32),
            jax.ShapeDtypeStruct((users, rank), f32),
            jax.ShapeDtypeStruct((users, rank), bf16),
            jax.ShapeDtypeStruct((sizes[0], rank), f32),
            jax.ShapeDtypeStruct((users, sizes[0]), bf16),
            jax.ShapeDtypeStruct((2, blocks, users, 2, LANES), bf16),
            *[jax.ShapeDtypeStruct((size, rank), f32) for size in sizes],
        ),
        [HBM] * 6,
        (VMEM,) * (8 + count),
        8 * users * items * GROUP,
        [
            pltpu.SMEM((tiles, strata), jnp.int32),
            pltpu.SMEM((1, strata), jnp.int32),
            pltpu.SemaphoreType.DMA((2, blocks)),
            pltpu.SemaphoreType.DMA((3 + count,)),
        ],
    )(
        hbm(tile_list[0].T), hbm(tile_count), hbm(user_factors), hbm(item_factors),
        hbm(view(ratings)), hbm(view(weights)),
    )
    return *outs[:8], list(outs[8:])


def sort_strata(chosen, ratings, weights, mask):
    users, strata, items = ratings.shape
    rows = CHUNK * strata
    kept = len(chosen)

    def kernel(rating_ref, weight_ref, mask_ref, rating_out, weight_out):
        target = lax.broadcasted_iota(jnp.int32, (CHUNK * kept, rows), 0)
        source = lax.broadcasted_iota(jnp.int32, (CHUNK * kept, rows), 1)
        wanted = (target % CHUNK) * strata + target // CHUNK + chosen[0]
        pick = jnp.where(source == wanted, 1.0, 0.0).astype(bf16)
        for first in range(0, users, CHUNK):
            mine = slice(first * strata, first * strata + rows)
            into = slice(first, first + CHUNK)
            rating = jnp.dot(pick, rating_ref[mine, :], preferred_element_type=f32)
            weight = jnp.dot(pick, weight_ref[mine, :], preferred_element_type=f32)
            for index, stratum in enumerate(chosen):
                part = slice(index * CHUNK, (index + 1) * CHUNK)
                rating_out[index, into, :] = rating[part].astype(bf16)
                weight_out[index, into, :] = (weight[part] * mask_ref[stratum : stratum + 1, :]).astype(bf16)

    table = jax.ShapeDtypeStruct((kept, users, items), bf16)
    return call(
        kernel, (table, table), [VMEM] * 3, (VMEM, VMEM), 4 * kept * users * items * rows
    )(ratings.reshape(users * strata, items), weights.reshape(users * strata, items), mask)


def piece_step(user_half, rows, rating_ref, weight_ref, stratum, cols):
    predicted = lax.dot_general(user_half, rows.astype(bf16), RANK, preferred_element_type=f32)
    rating = rating_ref[stratum, :, cols].astype(f32)
    weight = weight_ref[stratum, :, cols].astype(f32)
    residual = (weight * (predicted - rating)).astype(bf16)
    grad = lax.dot_general(residual, user_half, USERS, preferred_element_type=f32)
    return residual, rows - learn_rate * (grad + ridge_weight * rows)


def users_grad(residual, rows):
    return jnp.dot(residual, rows.astype(bf16), preferred_element_type=f32)


def first_piece(stratum, cols, user_half, piece, ratings, weights):
    def kernel(half_ref, piece_ref, rating_ref, weight_ref, new_ref, residual_ref):
        residual_ref[...], new_ref[...] = piece_step(
            half_ref[...], piece_ref[...], rating_ref, weight_ref, stratum, cols
        )

    users = user_half.shape[0]
    m, rank = piece.shape
    return call(
        kernel,
        (jax.ShapeDtypeStruct((m, rank), f32), jax.ShapeDtypeStruct((users, m), bf16)),
        [VMEM] * 4,
        (VMEM, VMEM),
        4 * users * m * rank,
    )(user_half, piece, ratings, weights)


def users_step(user_rows, residuals, pieces):
    count = len(pieces)

    def kernel(user_ref, *refs):
        residual_refs, piece_refs, (user_out, half_out) = refs[:count], refs[count : 2 * count], refs[2 * count :]
        user = user_ref[...]
        grad = ridge_weight * user
        for residual_ref, piece_ref in zip(residual_refs, piece_refs):
            grad += users_grad(residual_ref[...], piece_ref[...])
        user = user - learn_rate * grad
        user_out[...] = user
        half_out[...] = user.astype(bf16)

    users, rank = user_rows.shape
    return call(
        kernel,
        (jax.ShapeDtypeStruct((users, rank), f32), jax.ShapeDtypeStruct((users, rank), bf16)),
        [VMEM] * (1 + 2 * count),
        (VMEM, VMEM),
        2 * users * rank * users,
    )(user_rows, *residuals, *pieces)


def middle_piece(stratum, cols, user_rows, user_half, piece, ratings, weights, earlier):
    def kernel(user_ref, half_ref, piece_ref, rating_ref, weight_ref, *refs):
        earlier_refs, (new_ref, grad_ref) = refs[:-2], refs[-2:]
        rows = piece_ref[...]
        residual, new_ref[...] = piece_step(half_ref[...], rows, rating_ref, weight_ref, stratum, cols)
        if len(earlier_refs) == 2:
            grad = ridge_weight * user_ref[...] + users_grad(earlier_refs[1][...], earlier_refs[0][...])
        else:
            grad = earlier_refs[0][...]
        grad_ref[...] = grad + users_grad(residual, rows)

    users = user_half.shape[0]
    m, rank = piece.shape
    return call(
        kernel,
        (jax.ShapeDtypeStruct((m, rank), f32), jax.ShapeDtypeStruct((users, rank), f32)),
        [VMEM] * (5 + len(earlier)),
        (VMEM, VMEM),
        8 * users * m * rank,
    )(user_rows, user_half, piece, ratings, weights, *earlier)


def finish(stratum, cols, user_rows, user_half, grad, piece, ratings, weights, news):
    m, rank = piece.shape
    users = user_rows.shape[0]
    done = len(news)

    def kernel(user_ref, half_ref, grad_ref, piece_ref, rating_ref, weight_ref, *refs):
        new_refs, (users_out, items_out, last_items, last_users, sems) = refs[:done], refs[done:]
        copies = []

        def write(source, target):
            copies.append(pltpu.make_async_copy(source, target, sems.at[len(copies)]))
            copies[-1].start()

        start = 0
        for new_ref in new_refs:
            write(new_ref, items_out.at[pl.ds(start, new_ref.shape[0])])
            start += new_ref.shape[0]
        rows = piece_ref[...]
        residuals = []
        for part in range(2):
            mine = slice(part * users // 2, (part + 1) * users // 2)
            predicted = lax.dot_general(half_ref[mine, :], rows.astype(bf16), RANK, preferred_element_type=f32)
            rating = rating_ref[stratum, mine, cols].astype(f32)
            weight = weight_ref[stratum, mine, cols].astype(f32)
            residuals.append((weight * (predicted - rating)).astype(bf16))
            last_users[mine, :] = user_ref[mine, :] - learn_rate * (
                grad_ref[mine, :] + users_grad(residuals[-1], rows)
            )
            span = pl.ds(part * users // 2, users // 2)
            write(last_users.at[span], users_out.at[span])
        residual = jnp.concatenate(residuals, axis=0)
        grad = lax.dot_general(residual, half_ref[...], USERS, preferred_element_type=f32)
        last_items[...] = rows - learn_rate * (grad + ridge_weight * rows)
        write(last_items, items_out.at[pl.ds(start, m)])
        for copy in copies:
            copy.wait()

    items = m + sum(new.shape[0] for new in news)
    return call(
        kernel,
        (jax.ShapeDtypeStruct((users, rank), f32), jax.ShapeDtypeStruct((items, rank), f32)),
        [VMEM] * (6 + done),
        (HBM, HBM),
        6 * users * m * rank,
        [
            pltpu.VMEM((m, rank), f32),
            pltpu.VMEM((users, rank), f32),
            pltpu.SemaphoreType.DMA((done + 3,)),
        ],
    )(user_rows, user_half, grad, piece, ratings, weights, *news)


def local(user_factors, item_factors, ratings, weights, tile_list, tile_count):
    starts, sizes = cut(item_factors.shape[0])
    cols = [slice(start, start + size) for start, size in zip(starts, sizes)]
    last = len(sizes) - 1
    rating_01, weight_01, mask, user_rows, user_half, *opened, raw, pieces = load(
        user_factors, item_factors, ratings, weights, tile_list, tile_count
    )
    tables = [(0, rating_01, weight_01), (1, rating_01, weight_01)]
    for chosen in LATER:
        sorted_ratings, sorted_weights = sort_strata(chosen, ratings, weights, mask)
        tables.extend((index, sorted_ratings, sorted_weights) for index in range(len(chosen)))
    for outer_step in range(S_OUT):
        for inner_step in range(S_IN):
            stratum = outer_step * S_IN + inner_step
            row, rating, weight = tables[stratum]

            def move(new):
                return move_items(new, outer_step, inner_step)

            final = stratum == S_OUT * S_IN - 1
            news, residuals = [], []
            if final:
                new, residual = first_piece(row, cols[0], user_half, pieces[0], rating, weight)
                news = [new]
                earlier = (pieces[0], residual)
                for j in range(1, last):
                    new, grad = middle_piece(row, cols[j], user_rows, user_half, pieces[j], rating, weight, earlier)
                    news.append(new)
                    earlier = (grad,)
                return finish(row, cols[last], user_rows, user_half, grad, pieces[last], rating, weight, news)
            for j in range(last + 1):
                if stratum == 0 and j == 0:
                    new, residual = opened
                else:
                    new, residual = first_piece(row, cols[j], user_half, pieces[j], rating, weight)
                residuals.append(residual)
                news.append(move(new))
                if stratum == 0 and j == 1:
                    rating, weight = sort_rest(raw, mask, rating, weight, 2 * sizes[0] // LANES, residual)
                    tables[:2] = [(0, rating, weight), (1, rating, weight)]
            user_rows, user_half = users_step(user_rows, residuals, pieces)
            pieces = news


def solution(mesh):
    in_specs = (
        P(("outer", "inner"), None),
        P(("outer", "inner"), None),
        P(("outer", "inner"), None, None),
        P(("outer", "inner"), None, None),
        P(("outer", "inner"), None, None),
        P(("outer", "inner"), None),
    )
    out_specs = (P(("outer", "inner"), None), P(("outer", "inner"), None))

    return jax.shard_map(local, mesh=mesh, in_specs=in_specs, out_specs=out_specs, check_vma=False)
```
